32 devices in a mesh: row: 4 (over y, core), col: 8 (over z, x).
Axes of the slice: x: 2, y: 2, z: 4, core: 2. Of those that a mesh axis runs over, the one named last changes fastest.
Arguments:
- ainv_top: float32 [4096, 4096], P('row', 'col'), may hold values from -0.25 to 0.25
- par_struct: int32 [8, 16], replicated, may hold values from 0 to 31, as said below
- par_panel: float32 [8, 16, 128, 128], P('col', 'row'), may hold values from -6 to 6
- par_linv: float32 [8, 128, 128], P('col', 'row'), may hold values from -0.0625 to 0.0625
- par_dinv: float32 [8, 128, 128], P('col', 'row'), may hold values from -192 to 192
- kid_panel: float32 [16, 16, 128, 128], P('col', 'row'), may hold values from -6 to 6
- kid_upper: float32 [16, 128, 128], P('col', 'row'), may hold values from -6 to 6
- kid_linv: float32 [16, 128, 128], P('col', 'row'), may hold values from -0.0625 to 0.0625
- kid_dinv: float32 [16, 128, 128], P('col', 'row'), may hold values from -192 to 192
Outputs:
- par_offdiag: float32 [8, 16, 128, 128], P('col', 'row')
- par_diag: float32 [8, 128, 128], P('col', 'row')
- kid_offdiag: float32 [16, 16, 128, 128], P('col', 'row')
- kid_parent: float32 [16, 128, 128], P('col', 'row')
- kid_diag: float32 [16, 128, 128], P('col', 'row')
The draws below stay inside these ranges and needn't reach their ends.
Inputs may be any that keep to these rules, and one draw needn't show every extreme that they name: `par_struct`: in every row, entries 2j and 2j + 1 are two different ancestors among j * 4 to (j + 1) * 4 - 1.
All inputs are finite; a program needn't handle non-finite values.
Results may differ from the reference program's by a relative error of at most 0.00014.
Values sent between devices are 32-bit elements; how exact they have to be, the bound alone decides.
No kernel may reach another device: no remote copies, remote signals or barrier semaphores. Data moves between devices by JAX's collectives and lax.ppermute only.
A program may use at most 128 MiB of HBM per device.

```python
import jax
import jax.numpy as jnp
from jax import lax

BLK = 128
ANC_COL = 4
KIDS = 2
NA = 32
SLOTS = 16
NU = 8
NK = 16


def pick_pair(one_key):
    return jax.random.permutation(one_key, ANC_COL)[:2]


def draw_par_struct(key, part):
    blocks_per_row = SLOTS // 2
    key_list = jax.random.split(key, NU * blocks_per_row)
    picks = jax.vmap(pick_pair)(key_list).astype(jnp.int32)
    offsets = jnp.arange(NU * blocks_per_row, dtype=jnp.int32) % blocks_per_row * ANC_COL
    return (picks + offsets[:, None]).reshape(NU, SLOTS).astype(jnp.int32)


def block_scale(rng, extent, shards, low, top_value):
    gain = 1.0
    for axis_at, shards_of in shards:
        heights = jax.random.uniform(jax.random.fold_in(jax.random.fold_in(rng, 6), axis_at), (shards_of,), jnp.float32, low / len(shards), top_value / len(shards))
        gain = gain * jnp.repeat(jnp.exp(heights), extent[axis_at] // shards_of).reshape((-1,) + (1,) * (len(extent) - 1 - axis_at))
    return gain


def gaussian(stream_key, extent, scale, reach, cuts=(), kind=jnp.bfloat16):
    level = block_scale(stream_key, extent, cuts, -0.22, 0.18) if cuts else 1.0
    array = jax.random.normal(stream_key, extent, jnp.float32) * scale * level
    return jnp.minimum(jnp.maximum(array, -reach), reach).astype(kind)


def setup_inputs(seed: int = 0) -> dict:
    seeds = jax.random.split(jax.random.key(seed), 10)
    return {
        "ainv_top": gaussian(seeds[0], (NA * BLK, NA * BLK), (SLOTS * BLK // 4) ** -0.5, 0.25, ((0, 4), (1, 8)), jnp.float32),
        "par_struct": draw_par_struct(jax.random.fold_in(seeds[9], 71), 0),
        "par_panel": gaussian(seeds[2], (NU, SLOTS, BLK, BLK), 1.0, 6.0, ((0, 8), (1, 4)), jnp.float32),
        "par_linv": gaussian(seeds[3], (NU, BLK, BLK), (64 * BLK) ** -0.5, 0.0625, ((0, 8), (1, 4)), jnp.float32),
        "par_dinv": gaussian(seeds[4], (NU, BLK, BLK), 32.0, 192.0, ((0, 8), (1, 4)), jnp.float32),
        "kid_panel": gaussian(seeds[5], (NK, SLOTS, BLK, BLK), 1.0, 6.0, ((0, 8), (1, 4)), jnp.float32),
        "kid_upper": gaussian(seeds[6], (NK, BLK, BLK), 1.0, 6.0, ((0, 8), (1, 4)), jnp.float32),
        "kid_linv": gaussian(seeds[7], (NK, BLK, BLK), (64 * BLK) ** -0.5, 0.0625, ((0, 8), (1, 4)), jnp.float32),
        "kid_dinv": gaussian(seeds[8], (NK, BLK, BLK), 32.0, 192.0, ((0, 8), (1, 4)), jnp.float32),
    }


highest = lax.Precision.HIGHEST


def reference(ainv_top, par_struct, par_panel, par_linv, par_dinv, kid_panel, kid_upper, kid_linv, kid_dinv):
    tile_view = ainv_top.reshape(NA, BLK, NA, BLK)

    def one_parent(packed):
        ancestors, panel, linv, dinv, kpanel, kupper, klinv, kdinv = packed
        ancestor_block = tile_view[ancestors[:, None], :, ancestors[None, :], :]
        par_hat = jnp.einsum("sij,jk->sik", panel, linv, precision=highest)
        par_off = -jnp.einsum("stij,tjk->sik", ancestor_block, par_hat, precision=highest)
        pivot_term = jnp.einsum("ji,jk,kl->il", linv, dinv, linv, precision=highest)
        par_diag = pivot_term - jnp.einsum("sji,sjk->ik", par_hat, par_off, precision=highest)
        kid_hat = jnp.einsum("csij,cjk->csik", kpanel, klinv, precision=highest)
        kid_uphat = jnp.einsum("cij,cjk->cik", kupper, klinv, precision=highest)
        kid_off = -(jnp.einsum("stij,ctjk->csik", ancestor_block, kid_hat, precision=highest)
                    + jnp.einsum("sij,cjk->csik", par_off, kid_uphat, precision=highest))
        kid_par = -(jnp.einsum("tji,ctjk->cik", par_off, kid_hat, precision=highest)
                    + jnp.einsum("ij,cjk->cik", par_diag, kid_uphat, precision=highest))
        kid_pivot = jnp.einsum("cji,cjk,ckl->cil", klinv, kdinv, klinv, precision=highest)
        kid_diag = (kid_pivot - jnp.einsum("csji,csjk->cik", kid_hat, kid_off, precision=highest)
                    - jnp.einsum("cji,cjk->cik", kid_uphat, kid_par, precision=highest))
        return par_off, par_diag, kid_off, kid_par, kid_diag

    packed = (par_struct, par_panel, par_linv, par_dinv,
              kid_panel.reshape(NU, KIDS, SLOTS, BLK, BLK),
              kid_upper.reshape(NU, KIDS, BLK, BLK),
              kid_linv.reshape(NU, KIDS, BLK, BLK),
              kid_dinv.reshape(NU, KIDS, BLK, BLK))
    par_off, par_diag, kid_off, kid_par, kid_diag = lax.map(one_parent, packed)
    return (par_off, par_diag, kid_off.reshape(NK, SLOTS, BLK, BLK),
            kid_par.reshape(NK, BLK, BLK), kid_diag.reshape(NK, BLK, BLK))
```

```python
import jax
import jax.numpy as jnp
from jax import lax
from jax.sharding import PartitionSpec as P

high = lax.Precision.HIGH
highest = lax.Precision.HIGHEST


def mm(spec, *operands, precision=high):
    return jnp.einsum(spec, *operands, precision=precision)


def on_device(
    ainv_top, par_struct, par_panel, par_linv, par_dinv, kid_panel, kid_upper, kid_linv, kid_dinv
):
    grid_rows = lax.axis_size("row")
    grid_cols = lax.axis_size("col")
    my_row = lax.axis_index("row")
    my_col = lax.axis_index("col")
    width = par_panel.shape[-1]
    band_rows = width // grid_rows
    slot_share = par_panel.shape[1]
    children = kid_panel.shape[0]
    pair_width = par_struct.shape[1] // grid_cols
    tile_rows = ainv_top.shape[0] // width
    tile_cols = ainv_top.shape[1] // width

    local_tiles = ainv_top.reshape(tile_rows, width, tile_cols, width)
    pick_rows = lax.dynamic_slice_in_dim(par_struct, my_row * slot_share, slot_share, 1)
    pick_cols = lax.dynamic_slice_in_dim(par_struct, my_col * pair_width, pair_width, 1)
    pick_rows = pick_rows - my_row * tile_rows
    pick_cols = pick_cols - my_col * tile_cols
    tiles = local_tiles[pick_rows[:, :, None], :, pick_cols[:, None, :], :]

    small = jnp.concatenate([par_linv, par_dinv, kid_upper, kid_linv, kid_dinv], axis=0)
    small = lax.all_gather(small, "row", axis=1, tiled=True)
    plinv, pdinv = small[0], small[1]
    kupper = small[2 : 2 + children]
    klinv = small[2 + children : 2 + 2 * children]
    kdinv = small[2 + 2 * children :]
    panels = jnp.concatenate([par_panel, kid_panel], axis=0)
    every = lax.all_gather(panels, "row", axis=1, tiled=True)

    moved = lax.all_to_all(tiles, "col", 0, 0, tiled=True)
    every = every.reshape(1 + children, grid_cols, pair_width, width, width)
    prod = mm("cjkab,nckbd->njad", moved, every)

    par_off = -mm("jab,bc->jac", prod[0], plinv)
    par_hat = mm("jab,bc->jac", par_panel[0], plinv)
    kid_hat = mm("njab,nbc->njac", kid_panel, klinv)
    kuphat = mm("nab,nbc->nac", kupper, klinv)
    kid_sum = prod[1:] + mm("jab,nbc->njac", par_off, kupper)
    kid_off = -mm("njab,nbc->njac", kid_sum, klinv)

    diag_part = mm("jba,jbc->ac", par_hat, par_off)
    parent_part = mm("jba,njbc->nac", par_off, kid_hat)
    hat_part = mm("njba,njbc->nac", kid_hat, kid_off)
    inner = parent_part - mm("ab,nbc->nac", diag_part, kuphat)
    edge_part = mm("nba,nbc->nac", kuphat, inner) - hat_part
    parts = jnp.concatenate([diag_part[None], parent_part, edge_part], axis=0)
    parts = parts.reshape(1 + 2 * children, grid_rows, band_rows, width)
    parts = lax.all_to_all(parts, "row", 1, 1, tiled=True)
    sums = parts.sum(axis=1)

    par_pivot = mm("ba,bc,cd->ad", plinv, pdinv, plinv)
    kid_pivot = mm("nba,nbc,ncd->nad", klinv, kdinv, klinv)
    kid_pivot = kid_pivot + mm("nba,bc,ncd->nad", kuphat, par_pivot, kuphat)
    start = my_row * band_rows
    par_diag = lax.dynamic_slice_in_dim(par_pivot, start, band_rows, 0) - sums[0]
    kid_par = -(sums[1 : 1 + children] + mm("ab,nbc->nac", par_diag, kuphat))
    kid_diag = lax.dynamic_slice_in_dim(kid_pivot, start, band_rows, 1) + sums[1 + children :]
    return par_off[None], par_diag[None], kid_off, kid_par, kid_diag


def solution(mesh):
    placed = (
        P("row", "col"),
        P(),
        P("col", "row", None, None),
        P("col", "row", None),
        P("col", "row", None),
        P("col", "row", None, None),
        P("col", "row", None),
        P("col", "row", None),
        P("col", "row", None),
    )
    return jax.shard_map(
        on_device,
        mesh=mesh,
        in_specs=placed,
        out_specs=(
            P("col", "row", None, None),
            P("col", "row", None),
            P("col", "row", None, None),
            P("col", "row", None),
            P("col", "row", None),
        ),
        check_vma=False,
    )
```

```python
import functools

import jax
import jax.numpy as jnp
from jax import lax
from jax.experimental import pallas as pl
from jax.experimental.pallas import tpu as pltpu
from jax.sharding import PartitionSpec as P

highest = lax.Precision.HIGHEST
VMEM = pl.BlockSpec(memory_space=pltpu.VMEM)
SMEM = pl.BlockSpec(memory_space=pltpu.SMEM)


def mm(spec, *operands, precision=highest):
    return jnp.einsum(spec, *operands, precision=precision)


def swap(array, row_bits, col_bits):
    rows, cols = lax.axis_size("row"), lax.axis_size("col")
    pairs = [
        (r * cols + c, (r ^ row_bits) * cols + (c ^ col_bits))
        for r in range(rows)
        for c in range(cols)
    ]
    return lax.ppermute(array, ("row", "col"), pairs)


def pick_kernel(plan, place, struct, ainv, *outs):
    width, tile_rows, tile_cols = plan
    row, col, base = place[0], place[1], place[2]
    members, slot_share, pair_width = outs[0].shape[:3]
    for member in range(members):
        for side, out in enumerate(outs):
            u = jnp.bitwise_xor(base, (1 - side) * members) + member
            for k in range(pair_width):
                at_col = struct[u, col * pair_width + k] - col * tile_cols
                for j in range(slot_share):
                    at_row = struct[u, row * slot_share + j] - row * tile_rows
                    out[member, j, k] = ainv[
                        pl.ds(pl.multiple_of(at_row * width, width), width),
                        pl.ds(pl.multiple_of(at_col * width, width), width),
                    ]


def split(value):
    top = value.astype(jnp.bfloat16)
    return top, (value - top.astype(jnp.float32)).astype(jnp.bfloat16)


def product_kernel(start, place, tiles, *refs):
    panels, out = refs[:-1], refs[-1]
    members, slot_share, pair_width, width, _ = tiles.shape
    count, halves = out.shape[0], panels[0].shape[0]
    lhs, rhs = [], []
    for member in range(members):
        at = jnp.bitwise_xor(place[0], member)
        for k in range(pair_width):
            lhs.append(jnp.concatenate([tiles[member, j, k] for j in range(slot_share)], axis=0))
            blocks = []
            for n in range(start, start + count):
                block = panels[0][0, n, k]
                for d in range(1, members):
                    block = jnp.where(at == d, panels[d // halves][d % halves, n, k], block)
                blocks.append(block)
            rhs.append(jnp.concatenate(blocks, axis=1))
    lhs_top, lhs_rest = split(jnp.concatenate(lhs, axis=1))
    rhs_top, rhs_rest = split(jnp.concatenate(rhs, axis=0))
    dot = functools.partial(jnp.dot, preferred_element_type=jnp.float32)
    total = dot(lhs_top, rhs_rest) + dot(lhs_rest, rhs_top) + dot(lhs_top, rhs_top)
    for n in range(count):
        for j in range(slot_share):
            out[n, j] = total[j * width : (j + 1) * width, n * width : (n + 1) * width]


def product(place, tiles, panels, start, stop):
    members, slot_share, pair_width, width, _ = tiles.shape
    count = stop - start
    flops = 6 * members * pair_width * slot_share * count * width**3
    return pl.pallas_call(
        functools.partial(product_kernel, start),
        out_shape=jax.ShapeDtypeStruct((count, slot_share, width, width), jnp.float32),
        in_specs=[SMEM] + [VMEM] * (1 + len(panels)),
        out_specs=VMEM,
        compiler_params=pltpu.CompilerParams(vmem_limit_bytes=40 * 2**20),
        cost_estimate=pl.CostEstimate(flops=flops, bytes_accessed=4 * 2**20, transcendentals=0),
    )(place, tiles, *panels)


def after(value, *earlier):
    return lax.optimization_barrier((value, *earlier))[0]


def on_device(
    ainv_top, par_struct, par_panel, par_linv, par_dinv, kid_panel, kid_upper, kid_linv, kid_dinv
):
    grid_rows, grid_cols = lax.axis_size("row"), lax.axis_size("col")
    my_row, my_col = lax.axis_index("row"), lax.axis_index("col")
    width = par_panel.shape[-1]
    band_rows = width // grid_rows
    slot_share = par_panel.shape[1]
    children = kid_panel.shape[0]
    pair_width = par_struct.shape[1] // grid_cols
    tile_rows = ainv_top.shape[0] // width
    tile_cols = ainv_top.shape[1] // width
    halves = grid_cols // grid_rows
    lows = grid_rows // 2
    far_bits = lows * halves
    my_high, my_lane = my_col // halves, my_col % halves
    top = my_row // lows
    match = top == my_high // lows

    def take(half):
        par = lax.dynamic_slice_in_dim(par_panel, half * pair_width, pair_width, 1)
        kid = lax.dynamic_slice_in_dim(kid_panel, half * pair_width, pair_width, 1)
        return jnp.concatenate([par, kid], axis=0)

    def gather(mine, theirs, *earlier):
        both = after(jnp.stack([mine, theirs]), *earlier)
        return [both] + [swap(both, d, 0) for d in range(1, lows)]

    sent, kept = take(1 - top), take(top)
    got = swap(sent, lows, 0)
    away, near = jnp.where(match, got, kept), jnp.where(match, kept, got)
    far = swap(away, 0, far_bits)
    near_other = swap(near, lows, 0)

    small = jnp.concatenate([par_linv, par_dinv, kid_upper, kid_linv, kid_dinv], axis=0)
    small_other = swap(after(small, got), lows, 0)
    far_other = swap(after(far, near_other, small_other), lows, 0)
    far_panels = gather(far, far_other)

    members = far_bits
    groups = [list(range(0, members)), list(range(members, 2 * members))]
    piece = jax.ShapeDtypeStruct((members, slot_share, pair_width, width, width), jnp.float32)
    far_tiles, near_tiles = pl.pallas_call(
        functools.partial(pick_kernel, (width, tile_rows, tile_cols)),
        out_shape=[piece] * 2,
        in_specs=[SMEM, SMEM, VMEM],
        out_specs=[VMEM] * 2,
        compiler_params=pltpu.CompilerParams(vmem_limit_bytes=24 * 2**20),
        cost_estimate=pl.CostEstimate(flops=0, bytes_accessed=6 * 2**20, transcendentals=0),
    )(jnp.stack([my_row, my_col, my_col // members * members]), par_struct, after(ainv_top, sent))
    far_tiles = lax.all_to_all(far_tiles, "col", 0, 0, axis_index_groups=groups, tiled=True)
    near_tiles = after(near_tiles, far_tiles, small_other)
    near_tiles = lax.all_to_all(near_tiles, "col", 0, 0, axis_index_groups=groups, tiled=True)

    place = ((my_row % lows) * halves + top).reshape(1)
    par_away = product(place, far_tiles, far_panels, 0, 1)
    par_back = swap(par_away, 0, far_bits)
    kid_back = swap(product(place, far_tiles, far_panels, 1, 1 + children), 0, far_bits)

    near_panels = gather(near, near_other, par_away)
    small, order, bit = jnp.stack([small, small_other]), [0, lows], lows // 2
    small = after(small, par_away)
    while bit:
        small = jnp.concatenate([small, swap(small, bit, 0)], axis=0)
        order += [d ^ bit for d in order]
        bit //= 2
    inverse = sorted(range(grid_rows), key=order.__getitem__)
    at = jnp.asarray(inverse)[jnp.arange(grid_rows) ^ my_row]
    small = small[at].swapaxes(0, 1).reshape(small.shape[1], width, width)

    sums = product(place, near_tiles, near_panels, 0, 1 + children)
    par_sum = sums[:1] + par_back
    kid_sum = sums[1:] + kid_back
    plinv, pdinv = small[0], small[1]
    kupper = small[2 : 2 + children]
    klinv = small[2 + children : 2 + 2 * children]
    kdinv = small[2 + 2 * children :]

    par_off = -mm("jab,bc->jac", par_sum[0], plinv)
    par_hat = mm("jab,bc->jac", par_panel[0], plinv)
    kid_hat = mm("njab,nbc->njac", kid_panel, klinv)
    kuphat = mm("nab,nbc->nac", kupper, klinv)
    kid_sum = kid_sum + mm("jab,nbc->njac", par_off, kupper)
    kid_off = -mm("njab,nbc->njac", kid_sum, klinv)

    diag_part = mm("jba,jbc->ac", par_hat, par_off)
    parent_part = mm("jba,njbc->nac", par_off, kid_hat)
    hat_part = mm("njba,njbc->nac", kid_hat, kid_off)
    inner = parent_part - mm("ab,nbc->nac", diag_part, kuphat)
    edge_part = mm("nba,nbc->nac", kuphat, inner) - hat_part
    terms = jnp.concatenate([diag_part[None], parent_part, edge_part], axis=0)
    terms = terms.reshape(1 + 2 * children, grid_rows, band_rows, width)
    sums = lax.dynamic_index_in_dim(terms, my_row, 1, keepdims=False)
    for d in range(1, grid_rows):
        sums += swap(lax.dynamic_index_in_dim(terms, my_row ^ d, 1, keepdims=False), d, 0)

    par_pivot = mm("ba,bc,cd->ad", plinv, pdinv, plinv)
    kid_pivot = mm("nba,nbc,ncd->nad", klinv, kdinv, klinv)
    kid_pivot = kid_pivot + mm("nba,bc,ncd->nad", kuphat, par_pivot, kuphat)
    start = my_row * band_rows
    par_diag = lax.dynamic_slice_in_dim(par_pivot, start, band_rows, 0) - sums[0]
    kid_par = -(sums[1 : 1 + children] + mm("ab,nbc->nac", par_diag, kuphat))
    kid_diag = lax.dynamic_slice_in_dim(kid_pivot, start, band_rows, 1) + sums[1 + children :]
    return par_off[None], par_diag[None], kid_off, kid_par, kid_diag


def solution(mesh):
    placed = (
        P("row", "col"),
        P(),
        P("col", "row", None, None),
        P("col", "row", None),
        P("col", "row", None),
        P("col", "row", None, None),
        P("col", "row", None),
        P("col", "row", None),
        P("col", "row", None),
    )
    return jax.shard_map(
        on_device,
        mesh=mesh,
        in_specs=placed,
        out_specs=(
            P("col", "row", None, None),
            P("col", "row", None),
            P("col", "row", None, None),
            P("col", "row", None),
            P("col", "row", None),
        ),
        check_vma=False,
    )
```

```python
import functools

import jax
import jax.numpy as jnp
from jax import lax
from jax.experimental import pallas as pl
from jax.experimental.pallas import tpu as pltpu
from jax.sharding import PartitionSpec as P

highest = lax.Precision.HIGHEST
VMEM = pl.BlockSpec(memory_space=pltpu.VMEM)
SMEM = pl.BlockSpec(memory_space=pltpu.SMEM)


def mm(spec, *operands, precision=highest):
    return jnp.einsum(spec, *operands, precision=precision)


def swap(array, row_bits, col_bits):
    rows, cols = lax.axis_size("row"), lax.axis_size("col")
    pairs = [
        (r * cols + c, (r ^ row_bits) * cols + (c ^ col_bits))
        for r in range(rows)
        for c in range(cols)
    ]
    return lax.ppermute(array, ("row", "col"), pairs)


def pick_kernel(plan, place, struct, ainv, *outs):
    width, tile_rows, tile_cols = plan
    row, col, base = place[0], place[1], place[2]
    members, slot_share, pair_width = outs[0].shape[:3]
    for member in range(members):
        for side, out in enumerate(outs):
            u = jnp.bitwise_xor(base, (1 - side) * members) + member
            for k in range(pair_width):
                at_col = struct[u, col * pair_width + k] - col * tile_cols
                for j in range(slot_share):
                    at_row = struct[u, row * slot_share + j] - row * tile_rows
                    out[member, j, k] = ainv[
                        pl.ds(pl.multiple_of(at_row * width, width), width),
                        pl.ds(pl.multiple_of(at_col * width, width), width),
                    ]


def split(value):
    top = value.astype(jnp.bfloat16)
    return top, (value - top.astype(jnp.float32)).astype(jnp.bfloat16)


def product_kernel(plan, place, tiles, *refs):
    start, first, count_panels = plan
    panels, out = refs[:count_panels], refs[-1]
    members, slot_share, pair_width, width, _ = tiles.shape
    count = out.shape[0]
    lhs, rhs = [], []
    for i, panel in enumerate(panels):
        at = jnp.bitwise_xor(place[0], first + i)
        for k in range(pair_width):
            lhs.append(jnp.concatenate([tiles[at, j, k] for j in range(slot_share)], axis=0))
            blocks = [panel[n, k] for n in range(start, start + count)]
            rhs.append(jnp.concatenate(blocks, axis=1))
    lhs_top, lhs_rest = split(jnp.concatenate(lhs, axis=1))
    rhs_top, rhs_rest = split(jnp.concatenate(rhs, axis=0))
    mul = functools.partial(jnp.dot, preferred_element_type=jnp.float32)
    total = mul(lhs_top, rhs_rest) + mul(lhs_rest, rhs_top) + mul(lhs_top, rhs_top)
    for n in range(count):
        for j in range(slot_share):
            value = total[j * width : (j + 1) * width, n * width : (n + 1) * width]
            if len(refs) > count_panels + 1:
                value += refs[count_panels][start + n, j]
            out[n, j] = value


def product(place, tiles, panels, start, stop, first=0, so_far=()):
    members, slot_share, pair_width, width, _ = tiles.shape
    count = stop - start
    flops = 6 * len(panels) * pair_width * slot_share * count * width**3
    return pl.pallas_call(
        functools.partial(product_kernel, (start, first, len(panels))),
        out_shape=jax.ShapeDtypeStruct((count, slot_share, width, width), jnp.float32),
        in_specs=[SMEM] + [VMEM] * (1 + len(panels) + len(so_far)),
        out_specs=VMEM,
        compiler_params=pltpu.CompilerParams(vmem_limit_bytes=40 * 2**20),
        cost_estimate=pl.CostEstimate(flops=flops, bytes_accessed=4 * 2**20, transcendentals=0),
    )(place, tiles, *panels, *so_far)


def dot(a, b):
    return jnp.dot(a, b, precision=highest, preferred_element_type=jnp.float32)


def rows_of(ref, *at):
    slots = ref.shape[-3]
    return jnp.concatenate([ref[(*at, s)] for s in range(slots)], axis=0)


def parent_kernel(near, back, linv, upper, uphat, par_hat, kid_hat, off, part, kid_sum):
    slots, width = off.shape[1], off.shape[2]
    kids = upper.shape[0]
    value = -dot(rows_of(near, 0) + rows_of(back, 0), linv[...])
    turned = value.T
    diag = dot(rows_of(par_hat).T, value)
    part[0] = diag
    for s in range(slots):
        off[0, s] = value[s * width : (s + 1) * width]
    for c in range(kids):
        cross = dot(turned, rows_of(kid_hat, c))
        part[1 + c] = cross
        part[1 + kids + c] = dot(uphat[c].T, cross - dot(diag, uphat[c]))
        total = rows_of(near, 1 + c) + dot(value, upper[c])
        for s in range(slots):
            kid_sum[c, s] = total[s * width : (s + 1) * width]


def kid_kernel(place, kid_sum, back, linv, kid_hat, part, off, *bands):
    kids, slots, width, _ = off.shape
    height = bands[0].shape[1]
    bands, terms = bands[:-1], bands[-1]
    terms[...] = part[...]
    for c in range(kids):
        value = -dot(rows_of(kid_sum, c) + rows_of(back, c), linv[c])
        terms[1 + kids + c] = part[1 + kids + c] - dot(rows_of(kid_hat, c).T, value)
        for s in range(slots):
            off[c, s] = value[s * width : (s + 1) * width]
    for d, band in enumerate(bands):
        at = pl.multiple_of(jnp.bitwise_xor(place[0], d) * height, height)
        for i in range(terms.shape[0]):
            band[i] = terms[i, pl.ds(at, height), :]


def band_kernel(par_pivot, kid_pivot, uphat, *refs):
    bands, (par_diag, kid_par, kid_diag) = refs[:-3], refs[-3:]
    kids = uphat.shape[0]

    def total(i):
        return functools.reduce(lambda a, b: a + b, [band[i] for band in bands])

    diag = par_pivot[...] - total(0)
    par_diag[0] = diag
    for c in range(kids):
        kid_par[c] = -(total(1 + c) + dot(diag, uphat[c]))
        kid_diag[c] = kid_pivot[c] + total(1 + kids + c)


def local(kernel, shapes, *operands, scalars=0, scratch=()):
    return pl.pallas_call(
        kernel,
        out_shape=[jax.ShapeDtypeStruct(shape, jnp.float32) for shape in shapes],
        in_specs=[SMEM] * scalars + [VMEM] * (len(operands) - scalars),
        out_specs=[VMEM] * len(shapes),
        scratch_shapes=[pltpu.VMEM(shape, jnp.float32) for shape in scratch],
        compiler_params=pltpu.CompilerParams(vmem_limit_bytes=24 * 2**20),
        cost_estimate=pl.CostEstimate(flops=10**8, bytes_accessed=2 * 2**20, transcendentals=0),
    )(*operands)


def after(value, *earlier):
    return lax.optimization_barrier((value, *earlier))[0]


def on_device(
    ainv_top, par_struct, par_panel, par_linv, par_dinv, kid_panel, kid_upper, kid_linv, kid_dinv
):
    grid_rows, grid_cols = lax.axis_size("row"), lax.axis_size("col")
    my_row, my_col = lax.axis_index("row"), lax.axis_index("col")
    width = par_panel.shape[-1]
    band_rows = width // grid_rows
    slot_share = par_panel.shape[1]
    children = kid_panel.shape[0]
    pair_width = par_struct.shape[1] // grid_cols
    tile_rows = ainv_top.shape[0] // width
    tile_cols = ainv_top.shape[1] // width
    halves = grid_cols // grid_rows
    lows = grid_rows // 2
    far_bits = lows * halves
    my_high, my_lane = my_col // halves, my_col % halves
    top = my_row // lows
    match = top == my_high // lows

    def take(half):
        par = lax.dynamic_slice_in_dim(par_panel, half * pair_width, pair_width, 1)
        kid = lax.dynamic_slice_in_dim(kid_panel, half * pair_width, pair_width, 1)
        return jnp.concatenate([par, kid], axis=0)

    def gather(mine, theirs, *earlier):
        pieces = [mine, theirs]
        return pieces + [
            swap(after(piece, *earlier), d, 0) for d in range(1, lows) for piece in pieces
        ]

    sent, kept = take(1 - top), take(top)
    got = swap(sent, lows, 0)
    away, near = jnp.where(match, got, kept), jnp.where(match, kept, got)
    far = swap(away, 0, far_bits)
    near_other = swap(near, lows, 0)

    small = jnp.concatenate([par_linv, par_dinv, kid_upper, kid_linv, kid_dinv], axis=0)
    small_other = swap(after(small, got), lows, 0)
    far_other = swap(after(far, near_other, small_other), lows, 0)

    members = far_bits
    groups = [list(range(0, members)), list(range(members, 2 * members))]
    piece = jax.ShapeDtypeStruct((members, slot_share, pair_width, width, width), jnp.float32)
    far_tiles, near_tiles = pl.pallas_call(
        functools.partial(pick_kernel, (width, tile_rows, tile_cols)),
        out_shape=[piece] * 2,
        in_specs=[SMEM, SMEM, VMEM],
        out_specs=[VMEM] * 2,
        compiler_params=pltpu.CompilerParams(vmem_limit_bytes=24 * 2**20),
        cost_estimate=pl.CostEstimate(flops=0, bytes_accessed=6 * 2**20, transcendentals=0),
    )(jnp.stack([my_row, my_col, my_col // members * members]), par_struct, after(ainv_top, sent))
    far_tiles = lax.all_to_all(far_tiles, "col", 0, 0, axis_index_groups=groups, tiled=True)
    near_tiles = after(near_tiles, far_tiles, small_other)
    near_tiles = lax.all_to_all(near_tiles, "col", 0, 0, axis_index_groups=groups, tiled=True)

    place = ((my_row % lows) * halves + top).reshape(1)
    so_far = [product(place, far_tiles, [far], 0, 1 + children)]
    far_panels = gather(far, after(far_other, so_far[0]))
    so_far = [product(place, far_tiles, far_panels[1:-1], 0, 1 + children, 1, so_far)]
    last = (len(far_panels) - 1, so_far)
    par_away = product(place, far_tiles, far_panels[-1:], 0, 1, *last)
    par_back = swap(par_away, 0, far_bits)
    kid_away = product(place, far_tiles, far_panels[-1:], 1, 1 + children, *last)
    kid_back = swap(kid_away, 0, far_bits)

    near_panels = gather(near, near_other, kid_away)
    small, order, bit = jnp.stack([small, small_other]), [0, lows], lows // 2
    small = after(small, kid_away)
    while bit:
        small = jnp.concatenate([small, swap(small, bit, 0)], axis=0)
        order += [d ^ bit for d in order]
        bit //= 2
    inverse = sorted(range(grid_rows), key=order.__getitem__)
    at = jnp.asarray(inverse)[jnp.arange(grid_rows) ^ my_row]
    small = small[at].swapaxes(0, 1).reshape(small.shape[1], width, width)

    sums = product(place, near_tiles, near_panels, 0, 1 + children)
    plinv, pdinv = small[0], small[1]
    kupper = small[2 : 2 + children]
    klinv = small[2 + children : 2 + 2 * children]
    kdinv = small[2 + 2 * children :]

    par_hat = mm("jab,bc->jac", par_panel[0], plinv)
    kid_hat = mm("njab,nbc->njac", kid_panel, klinv)
    kuphat = mm("nab,nbc->nac", kupper, klinv)
    start = my_row * band_rows
    par_pivot = mm("ba,bc,cd->ad", plinv, pdinv, plinv)
    kid_pivot = mm("nba,nbc,ncd->nad", klinv, kdinv, klinv)
    kid_pivot = kid_pivot + mm("nba,bc,ncd->nad", kuphat, par_pivot, kuphat)
    par_pivot = lax.dynamic_slice_in_dim(par_pivot, start, band_rows, 0)
    kid_pivot = lax.dynamic_slice_in_dim(kid_pivot, start, band_rows, 1)

    terms = (1 + 2 * children, width, width)
    par_off, part, kid_sum = local(
        parent_kernel,
        [par_panel.shape, terms, kid_panel.shape],
        sums, par_back, plinv, kupper, kuphat, par_hat, kid_hat,
    )
    band = (1 + 2 * children, band_rows, width)
    kid_off, *bands = local(
        kid_kernel,
        [kid_panel.shape] + [band] * grid_rows,
        my_row.reshape(1), kid_sum, kid_back, klinv, kid_hat, part,
        scalars=1,
        scratch=[terms],
    )
    bands = [bands[0]] + [swap(bands[d], d, 0) for d in range(1, grid_rows)]
    par_diag, kid_par, kid_diag = local(
        band_kernel, [par_dinv.shape, kid_dinv.shape, kid_dinv.shape],
        par_pivot, kid_pivot, kuphat, *bands,
    )
    return par_off, par_diag, kid_off, kid_par, kid_diag


def solution(mesh):
    placed = (
        P("row", "col"),
        P(),
        P("col", "row", None, None),
        P("col", "row", None),
        P("col", "row", None),
        P("col", "row", None, None),
        P("col", "row", None),
        P("col", "row", None),
        P("col", "row", None),
    )
    return jax.shard_map(
        on_device,
        mesh=mesh,
        in_specs=placed,
        out_specs=(
            P("col", "row", None, None),
            P("col", "row", None),
            P("col", "row", None, None),
            P("col", "row", None),
            P("col", "row", None),
        ),
        check_vma=False,
    )
```

```python
import functools

import jax
import jax.numpy as jnp
from jax import lax
from jax.experimental import pallas as pl
from jax.experimental.pallas import tpu as pltpu
from jax.sharding import PartitionSpec as P

highest = lax.Precision.HIGHEST
VMEM = pl.BlockSpec(memory_space=pltpu.VMEM)
SMEM = pl.BlockSpec(memory_space=pltpu.SMEM)


def mm(spec, *operands, precision=highest):
    return jnp.einsum(spec, *operands, precision=precision)


def swap(array, row_bits, col_bits):
    rows, cols = lax.axis_size("row"), lax.axis_size("col")
    pairs = [
        (r * cols + c, (r ^ row_bits) * cols + (c ^ col_bits))
        for r in range(rows)
        for c in range(cols)
    ]
    return lax.ppermute(array, ("row", "col"), pairs)


def pick_kernel(plan, place, struct, ainv, out):
    width, tile_rows, tile_cols, flip = plan
    row, col, base = place[0], place[1], place[2]
    members, slot_share, pair_width = out.shape[:3]
    for member in range(members):
        u = jnp.bitwise_xor(base, flip) + member
        for k in range(pair_width):
            at_col = struct[u, col * pair_width + k] - col * tile_cols
            for j in range(slot_share):
                at_row = struct[u, row * slot_share + j] - row * tile_rows
                out[member, j, k] = ainv[
                    pl.ds(pl.multiple_of(at_row * width, width), width),
                    pl.ds(pl.multiple_of(at_col * width, width), width),
                ]


def split(value):
    top = value.astype(jnp.bfloat16)
    return top, (value - top.astype(jnp.float32)).astype(jnp.bfloat16)


def product_of(tiles, panels, start, count):
    slot_share, pair_width = tiles[0].shape[:2]
    lhs, rhs = [], []
    for tile, panel in zip(tiles, panels):
        for k in range(pair_width):
            lhs.append(jnp.concatenate([tile[j, k] for j in range(slot_share)], axis=0))
            blocks = [panel[n, k] for n in range(start, start + count)]
            rhs.append(jnp.concatenate(blocks, axis=1))
    lhs_top, lhs_rest = split(jnp.concatenate(lhs, axis=1))
    rhs_top, rhs_rest = split(jnp.concatenate(rhs, axis=0))
    mul = functools.partial(jnp.dot, preferred_element_type=jnp.float32)
    return mul(lhs_top, rhs_rest) + mul(lhs_rest, rhs_top) + mul(lhs_top, rhs_top)


def product_kernel(plan, place, *refs):
    start, used = plan
    tiles, panels, out = [ref.at[0] for ref in refs[:used]], refs[used : 2 * used], refs[-1]
    count, slot_share, width, _ = out.shape
    total = product_of(tiles, panels, start, count)
    for n in range(count):
        for j in range(slot_share):
            value = total[j * width : (j + 1) * width, n * width : (n + 1) * width]
            if len(refs) > 2 * used + 1:
                value += refs[2 * used][start + n, j]
            out[n, j] = value


def product(place, tiles, panels, start, stop, first=0, so_far=()):
    _, slot_share, pair_width, width, _ = tiles.shape
    count = stop - start
    result = (count, slot_share, width, width)
    flops = 6 * len(panels) * pair_width * slot_share * count * width**3

    def member(i):
        return lambda _, place: (jnp.bitwise_xor(place[0], first + i), 0, 0, 0, 0)

    whole = [pl.BlockSpec(a.shape, lambda *_: (0, 0, 0, 0)) for a in (*panels, *so_far)]
    return pl.pallas_call(
        functools.partial(product_kernel, (start, len(panels))),
        out_shape=jax.ShapeDtypeStruct(result, jnp.float32),
        grid_spec=pltpu.PrefetchScalarGridSpec(
            num_scalar_prefetch=1,
            grid=(1,),
            in_specs=[pl.BlockSpec((1, *tiles.shape[1:]), member(i)) for i in range(len(panels))]
            + whole,
            out_specs=pl.BlockSpec(result, lambda *_: (0, 0, 0, 0)),
        ),
        compiler_params=pltpu.CompilerParams(vmem_limit_bytes=40 * 2**20),
        cost_estimate=pl.CostEstimate(flops=flops, bytes_accessed=4 * 2**20, transcendentals=0),
    )(place, *[tiles] * len(panels), *panels, *so_far)


def dot(a, b):
    return jnp.dot(a, b, precision=highest, preferred_element_type=jnp.float32)


def rows_of(ref, *at):
    slots = ref.shape[-3]
    return jnp.concatenate([ref[(*at, s)] for s in range(slots)], axis=0)


def parent_kernel(place, tiles, back, linv, upper, uphat, par_hat, kid_hat, *refs):
    panels, (off, part, kid_sum) = refs[:-3], refs[-3:]
    slots, width = off.shape[1], off.shape[2]
    kids = upper.shape[0]
    nears = [tiles.at[jnp.bitwise_xor(place[0], i)] for i in range(len(panels))]
    near = product_of(nears, panels, 0, 1 + kids)
    value = -dot(near[:, :width] + rows_of(back, 0), linv[...])
    turned = value.T
    diag = dot(rows_of(par_hat).T, value)
    part[0] = diag
    for s in range(slots):
        off[0, s] = value[s * width : (s + 1) * width]
    for c in range(kids):
        cross = dot(turned, rows_of(kid_hat, c))
        part[1 + c] = cross
        part[1 + kids + c] = dot(uphat[c].T, cross - dot(diag, uphat[c]))
        total = near[:, (1 + c) * width : (2 + c) * width] + dot(value, upper[c])
        for s in range(slots):
            kid_sum[c, s] = total[s * width : (s + 1) * width]


def kid_kernel(place, kid_sum, back, linv, kid_hat, part, off, *bands):
    kids, slots, width, _ = off.shape
    height = bands[0].shape[1]
    bands, terms = bands[:-1], bands[-1]
    terms[...] = part[...]
    for c in range(kids):
        value = -dot(rows_of(kid_sum, c) + rows_of(back, c), linv[c])
        terms[1 + kids + c] = part[1 + kids + c] - dot(rows_of(kid_hat, c).T, value)
        for s in range(slots):
            off[c, s] = value[s * width : (s + 1) * width]
    for d, band in enumerate(bands):
        at = pl.multiple_of(jnp.bitwise_xor(place[0], d) * height, height)
        for i in range(terms.shape[0]):
            band[i] = terms[i, pl.ds(at, height), :]


def band_kernel(par_pivot, kid_pivot, uphat, *refs):
    bands, (par_diag, kid_par, kid_diag) = refs[:-3], refs[-3:]
    kids = uphat.shape[0]

    def total(i):
        return functools.reduce(lambda a, b: a + b, [band[i] for band in bands])

    diag = par_pivot[...] - total(0)
    par_diag[0] = diag
    for c in range(kids):
        kid_par[c] = -(total(1 + c) + dot(diag, uphat[c]))
        kid_diag[c] = kid_pivot[c] + total(1 + kids + c)


def local(kernel, shapes, *operands, scalars=0, scratch=()):
    return pl.pallas_call(
        kernel,
        out_shape=[jax.ShapeDtypeStruct(shape, jnp.float32) for shape in shapes],
        in_specs=[SMEM] * scalars + [VMEM] * (len(operands) - scalars),
        out_specs=[VMEM] * len(shapes),
        scratch_shapes=[pltpu.VMEM(shape, jnp.float32) for shape in scratch],
        compiler_params=pltpu.CompilerParams(vmem_limit_bytes=40 * 2**20),
        cost_estimate=pl.CostEstimate(flops=10**8, bytes_accessed=2 * 2**20, transcendentals=0),
    )(*operands)


def after(value, *earlier):
    return lax.optimization_barrier((value, *earlier))[0]


def on_device(
    ainv_top, par_struct, par_panel, par_linv, par_dinv, kid_panel, kid_upper, kid_linv, kid_dinv
):
    grid_rows, grid_cols = lax.axis_size("row"), lax.axis_size("col")
    my_row, my_col = lax.axis_index("row"), lax.axis_index("col")
    width = par_panel.shape[-1]
    band_rows = width // grid_rows
    slot_share = par_panel.shape[1]
    children = kid_panel.shape[0]
    pair_width = par_struct.shape[1] // grid_cols
    tile_rows = ainv_top.shape[0] // width
    tile_cols = ainv_top.shape[1] // width
    halves = grid_cols // grid_rows
    lows = grid_rows // 2
    far_bits = lows * halves
    my_high, my_lane = my_col // halves, my_col % halves
    top = my_row // lows
    match = top == my_high // lows

    members = far_bits
    groups = [list(range(0, members)), list(range(members, 2 * members))]
    piece = (members, slot_share, pair_width, width, width)
    spot = jnp.stack([my_row, my_col, my_col // members * members])

    def pick(flip, ainv):
        return pl.pallas_call(
            functools.partial(pick_kernel, (width, tile_rows, tile_cols, flip)),
            out_shape=jax.ShapeDtypeStruct(piece, jnp.float32),
            in_specs=[SMEM, SMEM, VMEM],
            out_specs=VMEM,
            compiler_params=pltpu.CompilerParams(vmem_limit_bytes=24 * 2**20),
            cost_estimate=pl.CostEstimate(flops=0, bytes_accessed=4 * 2**20, transcendentals=0),
        )(spot, par_struct, ainv)

    def exchange(tiles):
        return lax.all_to_all(tiles, "col", 0, 0, axis_index_groups=groups, tiled=True)

    def take(half):
        par = lax.dynamic_slice_in_dim(par_panel, half * pair_width, pair_width, 1)
        kid = lax.dynamic_slice_in_dim(kid_panel, half * pair_width, pair_width, 1)
        return jnp.concatenate([par, kid], axis=0)

    def gather(mine, theirs, *earlier):
        pieces = [mine, theirs]
        return pieces + [
            swap(after(piece, *earlier), d, 0) for d in range(1, lows) for piece in pieces
        ]

    sent, kept = take(1 - top), take(top)
    got = swap(sent, lows, 0)
    away, near = jnp.where(match, got, kept), jnp.where(match, kept, got)
    far = swap(away, 0, far_bits)
    near_other = swap(near, lows, 0)

    small = jnp.concatenate([par_linv, par_dinv, kid_upper, kid_linv, kid_dinv], axis=0)
    small_other = swap(after(small, got), lows, 0)
    far_tiles = exchange(pick(members, after(ainv_top, sent)))
    near_tiles = pick(0, after(ainv_top, got))
    far_other = swap(after(far, near_other, small_other, near_tiles), lows, 0)
    near_tiles = exchange(after(near_tiles, far_tiles, small_other))

    place = ((my_row % lows) * halves + top).reshape(1)
    so_far = [product(place, far_tiles, [far], 0, 1 + children)]
    far_panels = gather(far, after(far_other, so_far[0]))
    so_far = [product(place, far_tiles, far_panels[1:-1], 0, 1 + children, 1, so_far)]
    last = (len(far_panels) - 1, so_far)
    par_away = product(place, far_tiles, far_panels[-1:], 0, 1, *last)
    par_back = swap(par_away, 0, far_bits)
    last = (last[0], [after(so_far[0], par_away)])
    kid_away = product(place, far_tiles, far_panels[-1:], 1, 1 + children, *last)
    kid_back = swap(kid_away, 0, far_bits)

    near_panels = gather(near, near_other, kid_away)
    small, order, bit = jnp.stack([small, small_other]), [0, lows], lows // 2
    small = after(small, kid_away)
    while bit:
        small = jnp.concatenate([small, swap(small, bit, 0)], axis=0)
        order += [d ^ bit for d in order]
        bit //= 2
    inverse = sorted(range(grid_rows), key=order.__getitem__)
    at = jnp.asarray(inverse)[jnp.arange(grid_rows) ^ my_row]
    small = small[at].swapaxes(0, 1).reshape(small.shape[1], width, width)

    plinv, pdinv = small[0], small[1]
    kupper = small[2 : 2 + children]
    klinv = small[2 + children : 2 + 2 * children]
    kdinv = small[2 + 2 * children :]

    par_hat = mm("jab,bc->jac", par_panel[0], plinv)
    kid_hat = mm("njab,nbc->njac", kid_panel, klinv)
    kuphat = mm("nab,nbc->nac", kupper, klinv)
    start = my_row * band_rows
    par_pivot = mm("ba,bc,cd->ad", plinv, pdinv, plinv)
    kid_pivot = mm("nba,nbc,ncd->nad", klinv, kdinv, klinv)
    kid_pivot = kid_pivot + mm("nba,bc,ncd->nad", kuphat, par_pivot, kuphat)
    par_pivot = lax.dynamic_slice_in_dim(par_pivot, start, band_rows, 0)
    kid_pivot = lax.dynamic_slice_in_dim(kid_pivot, start, band_rows, 1)

    terms = (1 + 2 * children, width, width)
    par_off, part, kid_sum = local(
        parent_kernel,
        [par_panel.shape, terms, kid_panel.shape],
        place, near_tiles, par_back, plinv, kupper, kuphat, par_hat, kid_hat, *near_panels,
        scalars=1,
    )
    band = (1 + 2 * children, band_rows, width)
    kid_off, *bands = local(
        kid_kernel,
        [kid_panel.shape] + [band] * grid_rows,
        my_row.reshape(1), kid_sum, kid_back, klinv, kid_hat, part,
        scalars=1,
        scratch=[terms],
    )
    bands = [bands[0]] + [swap(bands[d], d, 0) for d in range(1, grid_rows)]
    par_diag, kid_par, kid_diag = local(
        band_kernel, [par_dinv.shape, kid_dinv.shape, kid_dinv.shape],
        par_pivot, kid_pivot, kuphat, *bands,
    )
    return par_off, par_diag, kid_off, kid_par, kid_diag


def solution(mesh):
    placed = (
        P("row", "col"),
        P(),
        P("col", "row", None, None),
        P("col", "row", None),
        P("col", "row", None),
        P("col", "row", None, None),
        P("col", "row", None),
        P("col", "row", None),
        P("col", "row", None),
    )
    return jax.shard_map(
        on_device,
        mesh=mesh,
        in_specs=placed,
        out_specs=(
            P("col", "row", None, None),
            P("col", "row", None),
            P("col", "row", None, None),
            P("col", "row", None),
            P("col", "row", None),
        ),
        check_vma=False,
    )
```

```python
import functools

import jax
import jax.numpy as jnp
from jax import lax
from jax.experimental import pallas as pl
from jax.experimental.pallas import tpu as pltpu
from jax.sharding import PartitionSpec as P

highest = lax.Precision.HIGHEST
VMEM = pl.BlockSpec(memory_space=pltpu.VMEM)
SMEM = pl.BlockSpec(memory_space=pltpu.SMEM)


def mm(spec, *operands, precision=highest):
    return jnp.einsum(spec, *operands, precision=precision)


def swap(array, row_bits, col_bits):
    rows, cols = lax.axis_size("row"), lax.axis_size("col")
    pairs = [
        (r * cols + c, (r ^ row_bits) * cols + (c ^ col_bits))
        for r in range(rows)
        for c in range(cols)
    ]
    return lax.ppermute(array, ("row", "col"), pairs)


def pick_kernel(plan, place, struct, ainv, out):
    width, tile_rows, tile_cols, flip = plan
    row, col, base = place[0], place[1], place[2]
    members, slot_share, pair_width = out.shape[:3]
    for member in range(members):
        u = jnp.bitwise_xor(base, flip) + member
        for k in range(pair_width):
            at_col = struct[u, col * pair_width + k] - col * tile_cols
            for j in range(slot_share):
                at_row = struct[u, row * slot_share + j] - row * tile_rows
                out[member, j, k] = ainv[
                    pl.ds(pl.multiple_of(at_row * width, width), width),
                    pl.ds(pl.multiple_of(at_col * width, width), width),
                ]


def split(value):
    top = value.astype(jnp.bfloat16)
    return top, (value - top.astype(jnp.float32)).astype(jnp.bfloat16)


def product_of(tiles, panels, start, count):
    slot_share, pair_width = tiles[0].shape[:2]
    lhs, rhs = [], []
    for tile, panel in zip(tiles, panels):
        for k in range(pair_width):
            lhs.append(jnp.concatenate([tile[j, k] for j in range(slot_share)], axis=0))
            blocks = [panel[n, k] for n in range(start, start + count)]
            rhs.append(jnp.concatenate(blocks, axis=1))
    return dot(jnp.concatenate(lhs, axis=1), jnp.concatenate(rhs, axis=0))


def product_kernel(plan, place, *refs):
    start, used = plan
    tiles, panels, out = [ref.at[0] for ref in refs[:used]], refs[used : 2 * used], refs[-1]
    count, slot_share, width, _ = out.shape
    total = product_of(tiles, panels, start, count)
    for n in range(count):
        for j in range(slot_share):
            value = total[j * width : (j + 1) * width, n * width : (n + 1) * width]
            if len(refs) > 2 * used + 1:
                value += refs[2 * used][start + n, j]
            out[n, j] = value


def product(place, tiles, panels, start, stop, first=0, so_far=()):
    _, slot_share, pair_width, width, _ = tiles.shape
    count = stop - start
    result = (count, slot_share, width, width)
    flops = 6 * len(panels) * pair_width * slot_share * count * width**3

    def member(i):
        return lambda _, place: (jnp.bitwise_xor(place[0], first + i), 0, 0, 0, 0)

    whole = [pl.BlockSpec(a.shape, lambda *_: (0, 0, 0, 0)) for a in (*panels, *so_far)]
    return pl.pallas_call(
        functools.partial(product_kernel, (start, len(panels))),
        out_shape=jax.ShapeDtypeStruct(result, jnp.float32),
        grid_spec=pltpu.PrefetchScalarGridSpec(
            num_scalar_prefetch=1,
            grid=(1,),
            in_specs=[pl.BlockSpec((1, *tiles.shape[1:]), member(i)) for i in range(len(panels))]
            + whole,
            out_specs=pl.BlockSpec(result, lambda *_: (0, 0, 0, 0)),
        ),
        compiler_params=pltpu.CompilerParams(vmem_limit_bytes=40 * 2**20),
        cost_estimate=pl.CostEstimate(flops=flops, bytes_accessed=4 * 2**20, transcendentals=0),
    )(place, *[tiles] * len(panels), *panels, *so_far)


def dot(a, b):
    (a_top, a_rest), (b_top, b_rest) = split(a), split(b)
    mul = functools.partial(jnp.dot, preferred_element_type=jnp.float32)
    return mul(a_top, b_rest) + mul(a_rest, b_top) + mul(a_top, b_top)


def rows_of(ref, *at):
    slots = ref.shape[-3]
    return jnp.concatenate([ref[(*at, s)] for s in range(slots)], axis=0)


def parent_kernel(place, tiles, back, linv, upper, uphat, par_hat, kid_hat, *refs):
    panels, (off, part, kid_sum) = refs[:-3], refs[-3:]
    slots, width = off.shape[1], off.shape[2]
    kids = upper.shape[0]
    nears = [tiles.at[jnp.bitwise_xor(place[0], i)] for i in range(len(panels))]
    near = product_of(nears, panels, 0, 1 + kids)
    value = -dot(near[:, :width] + rows_of(back, 0), linv[...])
    turned = value.T
    diag = dot(rows_of(par_hat).T, value)
    part[0] = diag
    for s in range(slots):
        off[0, s] = value[s * width : (s + 1) * width]
    for c in range(kids):
        cross = dot(turned, rows_of(kid_hat, c))
        part[1 + c] = cross
        part[1 + kids + c] = dot(uphat[c].T, cross - dot(diag, uphat[c]))
        total = near[:, (1 + c) * width : (2 + c) * width] + dot(value, upper[c])
        for s in range(slots):
            kid_sum[c, s] = total[s * width : (s + 1) * width]


def kid_kernel(place, kid_sum, back, linv, kid_hat, part, off, *bands):
    kids, slots, width, _ = off.shape
    height = bands[0].shape[1]
    bands, terms = bands[:-1], bands[-1]
    terms[...] = part[...]
    for c in range(kids):
        value = -dot(rows_of(kid_sum, c) + rows_of(back, c), linv[c])
        terms[1 + kids + c] = part[1 + kids + c] - dot(rows_of(kid_hat, c).T, value)
        for s in range(slots):
            off[c, s] = value[s * width : (s + 1) * width]
    for d, band in enumerate(bands):
        at = pl.multiple_of(jnp.bitwise_xor(place[0], d) * height, height)
        for i in range(terms.shape[0]):
            band[i] = terms[i, pl.ds(at, height), :]


def band_kernel(par_pivot, kid_pivot, uphat, *refs):
    bands, (par_diag, kid_par, kid_diag) = refs[:-3], refs[-3:]
    kids = uphat.shape[0]

    def total(i):
        return functools.reduce(lambda a, b: a + b, [band[i] for band in bands])

    diag = par_pivot[...] - total(0)
    par_diag[0] = diag
    for c in range(kids):
        kid_par[c] = -(total(1 + c) + dot(diag, uphat[c]))
        kid_diag[c] = kid_pivot[c] + total(1 + kids + c)


def local(kernel, shapes, *operands, scalars=0, scratch=()):
    return pl.pallas_call(
        kernel,
        out_shape=[jax.ShapeDtypeStruct(shape, jnp.float32) for shape in shapes],
        in_specs=[SMEM] * scalars + [VMEM] * (len(operands) - scalars),
        out_specs=[VMEM] * len(shapes),
        scratch_shapes=[pltpu.VMEM(shape, jnp.float32) for shape in scratch],
        compiler_params=pltpu.CompilerParams(vmem_limit_bytes=40 * 2**20),
        cost_estimate=pl.CostEstimate(flops=10**8, bytes_accessed=2 * 2**20, transcendentals=0),
    )(*operands)


def after(value, *earlier):
    return lax.optimization_barrier((value, *earlier))[0]


def on_device(
    ainv_top, par_struct, par_panel, par_linv, par_dinv, kid_panel, kid_upper, kid_linv, kid_dinv
):
    grid_rows, grid_cols = lax.axis_size("row"), lax.axis_size("col")
    my_row, my_col = lax.axis_index("row"), lax.axis_index("col")
    width = par_panel.shape[-1]
    band_rows = width // grid_rows
    slot_share = par_panel.shape[1]
    children = kid_panel.shape[0]
    pair_width = par_struct.shape[1] // grid_cols
    tile_rows = ainv_top.shape[0] // width
    tile_cols = ainv_top.shape[1] // width
    halves = grid_cols // grid_rows
    lows = grid_rows // 2
    far_bits = lows * halves
    my_high, my_lane = my_col // halves, my_col % halves
    top = my_row // lows
    match = top == my_high // lows

    members = far_bits
    groups = [list(range(0, members)), list(range(members, 2 * members))]
    piece = (members, slot_share, pair_width, width, width)
    spot = jnp.stack([my_row, my_col, my_col // members * members])

    def pick(flip, ainv):
        return pl.pallas_call(
            functools.partial(pick_kernel, (width, tile_rows, tile_cols, flip)),
            out_shape=jax.ShapeDtypeStruct(piece, jnp.float32),
            in_specs=[SMEM, SMEM, VMEM],
            out_specs=VMEM,
            compiler_params=pltpu.CompilerParams(vmem_limit_bytes=24 * 2**20),
            cost_estimate=pl.CostEstimate(flops=0, bytes_accessed=4 * 2**20, transcendentals=0),
        )(spot, par_struct, ainv)

    def exchange(tiles):
        return lax.all_to_all(tiles, "col", 0, 0, axis_index_groups=groups, tiled=True)

    def take(half):
        par = lax.dynamic_slice_in_dim(par_panel, half * pair_width, pair_width, 1)
        kid = lax.dynamic_slice_in_dim(kid_panel, half * pair_width, pair_width, 1)
        return jnp.concatenate([par, kid], axis=0)

    def gather(mine, theirs, *earlier):
        pieces = [mine, theirs]
        return pieces + [
            swap(after(piece, *earlier), d, 0) for d in range(1, lows) for piece in pieces
        ]

    sent, kept = take(1 - top), take(top)
    got = swap(sent, lows, 0)
    away, near = jnp.where(match, got, kept), jnp.where(match, kept, got)
    far = swap(away, 0, far_bits)
    near_other = swap(near, lows, 0)

    small = jnp.concatenate([par_linv, par_dinv, kid_upper, kid_linv, kid_dinv], axis=0)
    small_other = swap(after(small, got), lows, 0)
    far_tiles = exchange(pick(members, after(ainv_top, sent)))
    near_tiles = pick(0, after(ainv_top, got))
    far_other = swap(after(far, near_other, small_other, near_tiles), lows, 0)
    near_tiles = exchange(after(near_tiles, far_tiles, small_other))

    place = ((my_row % lows) * halves + top).reshape(1)
    so_far = [product(place, far_tiles, [far], 0, 1 + children)]
    far_panels = gather(far, after(far_other, so_far[0]))
    so_far = [product(place, far_tiles, far_panels[1:-1], 0, 1 + children, 1, so_far)]
    last = (len(far_panels) - 1, so_far)
    par_away = product(place, far_tiles, far_panels[-1:], 0, 1, *last)
    par_back = swap(par_away, 0, far_bits)
    last = (last[0], [after(so_far[0], par_away)])
    kid_away = product(place, far_tiles, far_panels[-1:], 1, 1 + children, *last)
    kid_back = swap(kid_away, 0, far_bits)

    near_panels = gather(near, near_other, kid_away)
    small, order, bit = jnp.stack([small, small_other]), [0, lows], lows // 2
    small = after(small, kid_away)
    while bit:
        small = jnp.concatenate([small, swap(small, bit, 0)], axis=0)
        order += [d ^ bit for d in order]
        bit //= 2
    inverse = sorted(range(grid_rows), key=order.__getitem__)
    at = jnp.asarray(inverse)[jnp.arange(grid_rows) ^ my_row]
    small = small[at].swapaxes(0, 1).reshape(small.shape[1], width, width)

    plinv, pdinv = small[0], small[1]
    kupper = small[2 : 2 + children]
    klinv = small[2 + children : 2 + 2 * children]
    kdinv = small[2 + 2 * children :]

    par_hat = mm("jab,bc->jac", par_panel[0], plinv)
    kid_hat = mm("njab,nbc->njac", kid_panel, klinv)
    kuphat = mm("nab,nbc->nac", kupper, klinv)
    start = my_row * band_rows
    par_pivot = mm("ba,bc,cd->ad", plinv, pdinv, plinv)
    kid_pivot = mm("nba,nbc,ncd->nad", klinv, kdinv, klinv)
    kid_pivot = kid_pivot + mm("nba,bc,ncd->nad", kuphat, par_pivot, kuphat)
    par_pivot = lax.dynamic_slice_in_dim(par_pivot, start, band_rows, 0)
    kid_pivot = lax.dynamic_slice_in_dim(kid_pivot, start, band_rows, 1)

    terms = (1 + 2 * children, width, width)
    par_off, part, kid_sum = local(
        parent_kernel,
        [par_panel.shape, terms, kid_panel.shape],
        place, near_tiles, par_back, plinv, kupper, kuphat, par_hat, kid_hat, *near_panels,
        scalars=1,
    )
    band = (1 + 2 * children, band_rows, width)
    kid_off, *bands = local(
        kid_kernel,
        [kid_panel.shape] + [band] * grid_rows,
        my_row.reshape(1), kid_sum, kid_back, klinv, kid_hat, part,
        scalars=1,
        scratch=[terms],
    )
    bands = [bands[0]] + [swap(bands[d], d, 0) for d in range(1, grid_rows)]
    par_diag, kid_par, kid_diag = local(
        band_kernel, [par_dinv.shape, kid_dinv.shape, kid_dinv.shape],
        par_pivot, kid_pivot, kuphat, *bands,
    )
    return par_off, par_diag, kid_off, kid_par, kid_diag


def solution(mesh):
    placed = (
        P("row", "col"),
        P(),
        P("col", "row", None, None),
        P("col", "row", None),
        P("col", "row", None),
        P("col", "row", None, None),
        P("col", "row", None),
        P("col", "row", None),
        P("col", "row", None),
    )
    return jax.shard_map(
        on_device,
        mesh=mesh,
        in_specs=placed,
        out_specs=(
            P("col", "row", None, None),
            P("col", "row", None),
            P("col", "row", None, None),
            P("col", "row", None),
            P("col", "row", None),
        ),
        check_vma=False,
    )
```
